256 devices in a mesh: subj: 4 (over y_hi, core), slab: 64 (over x, z, y_lo).
Axes of the slice: x: 4, y: 4 (y_hi: 2, y_lo: 2; y = y_hi * 2 + y_lo), z: 8, core: 2. Of those that a mesh axis runs over, the one named last changes fastest.
Arguments:
- momentum: bfloat16 [4, 3, 128, 256, 256], P('subj', None, 'slab'), may hold values from -6 to 6
- adjoint: bfloat16 [4, 128, 256, 256], P('subj', 'slab'), may hold values from -6 to 6
- code: int32 [4, 128, 256, 256], P('subj', 'slab'), may hold values from 0 to 4095
- template_grad: bfloat16 [3, 128, 256, 256], P(None, 'slab'), may hold values from -6 to 6
Outputs:
- alignment: bfloat16 [4, 128, 256, 256], P('subj', 'slab')
- template_update: float32 [128, 256, 256], P('slab', 'subj')
The draws below stay inside these ranges and needn't reach their ends.
Inputs may be any that keep to these rules, and one draw needn't show every extreme that they name: code // 256, (code // 16) % 16 and code % 16 are each 8 plus a displacement along z, y and x in quarter voxels.
All inputs are finite; a program needn't handle non-finite values.
Results may differ from the reference program's by a relative error of at most 0.012.
Values may be sent and summed in bfloat16 or wider, within the bound.
A program may use at most 128 MiB of HBM per device.

```python
import jax
import jax.numpy as jnp
from jax import lax

NX = 256
NY = 256
NZ = 128
SUBJECTS = 4


def set_ends(values, rng, least, top_value):
    shape = values.shape
    index_at = [jax.random.randint(jax.random.fold_in(rng, axis), (), 0, shape[axis]) for axis in range(len(shape))]
    values = values.at[tuple(index_at)].set(least)
    longest = shape.index(max(shape))
    index_at[longest] = (index_at[longest] + 1) % shape[longest]
    return values.at[tuple(index_at)].set(top_value)


def block_levels(key, dims, shards, low, top_value):
    def one(position, parts):
        draws = jax.random.uniform(jax.random.fold_in(jax.random.fold_in(key, 6), position), (parts,), jnp.float32, low / len(shards), top_value / len(shards))
        return jnp.repeat(jnp.exp(draws), dims[position] // parts).reshape((-1,) + (1,) * (len(dims) - position - 1))

    loudness = one(*shards[0])
    for cut in shards[1:]:
        loudness = loudness * one(*cut)
    return loudness


def centred(stream_key, dims, scale, limit, pieces=(), kind=jnp.bfloat16):
    array = jax.random.normal(stream_key, dims, jnp.float32) * scale
    if len(pieces) > 0:
        array = block_levels(stream_key, dims, pieces, -0.22, 0.18) * array
    return jnp.clip(array, min=-limit, max=limit).astype(kind)


def setup_inputs(seed: int = 0) -> dict:
    splits = jax.random.split(jax.random.key(seed), 5)
    return {
        "momentum": centred(splits[0], (SUBJECTS, 3, NZ, NY, NX), 1.0, 6.0, ((0, 4), (2, 64))),
        "adjoint": centred(splits[1], (SUBJECTS, NZ, NY, NX), 1.0, 6.0, ((0, 4), (1, 64))),
        "code": set_ends(jax.random.randint(splits[2], (SUBJECTS, NZ, NY, NX), 0, 4096), jax.random.fold_in(splits[2], 1), 0, 4095).astype(jnp.int32),
        "template_grad": centred(splits[3], (3, NZ, NY, NX), 1.0, 6.0, ((1, 64),)),
    }


rim = 2
bias = 8
decay = 8.0

def taps_matrix(rows, cols, offset):
    lags = jnp.arange(-15, 16, dtype=jnp.int32).astype(jnp.float32)
    scale = jnp.sqrt(jnp.sum(jnp.exp(-2.0 * jnp.abs(lags) / decay)))
    lag = jnp.arange(rows, dtype=jnp.int32)[:, None] - offset - jnp.arange(cols, dtype=jnp.int32)[None, :]
    dist = jnp.abs(lag).astype(jnp.float32)
    return jnp.where(jnp.abs(lag) <= 15, jnp.exp(-dist / decay) / scale, 0.0).astype(jnp.bfloat16)

def transport(framed, encoded):
    depth, height, breadth = encoded.shape
    rows_y = height + 2 * rim
    rows_x = breadth + 2 * rim
    flat = framed.reshape(-1)
    shift_z = encoded // 256 - bias
    shift_y = encoded // 16 % 16 - bias
    shift_x = encoded % 16 - bias
    whole_z = shift_z // 4
    whole_y = shift_y // 4
    whole_x = shift_x // 4
    frac_z = (shift_z - 4 * whole_z).astype(jnp.float32) * 0.25
    frac_y = (shift_y - 4 * whole_y).astype(jnp.float32) * 0.25
    frac_x = (shift_x - 4 * whole_x).astype(jnp.float32) * 0.25
    base = (jnp.arange(depth, dtype=jnp.int32)[:, None, None] + rim + whole_z) * (rows_y * rows_x)
    base = base + (jnp.arange(height, dtype=jnp.int32)[None, :, None] + rim + whole_y) * rows_x
    base = base + jnp.arange(breadth, dtype=jnp.int32)[None, None, :] + rim + whole_x
    pulled = jnp.zeros(encoded.shape, jnp.float32)
    for upper_z in (0, 1):
        weight_z = frac_z if upper_z else 1.0 - frac_z
        for upper_y in (0, 1):
            weight_y = frac_y if upper_y else 1.0 - frac_y
            for upper_x in (0, 1):
                weight_x = frac_x if upper_x else 1.0 - frac_x
                index = base + upper_z * (rows_y * rows_x) + upper_y * rows_x + upper_x
                values = jnp.take(flat, index)
                pulled = pulled + weight_z * weight_y * weight_x * values.astype(jnp.float32)
    return pulled

def reference(momentum, adjoint, code, template_grad):
    kernel_x = taps_matrix(NX, NX, 0)
    kernel_y = taps_matrix(NY, NY, 0)
    kernel_z = taps_matrix(NZ, NZ, 0)
    gradient = template_grad.astype(jnp.float32)
    padded = jnp.pad(adjoint, ((0, 0), (rim, rim), (rim, rim), (rim, rim)))

    def subject(total, item):
        moment, framed, encoded = item
        pulled = transport(framed, encoded)
        mixed = (moment.astype(jnp.float32) + pulled[None] * gradient).astype(jnp.bfloat16)
        along_x = jnp.dot(mixed.reshape(-1, NX), kernel_x, preferred_element_type=jnp.float32)
        along_x = along_x.astype(jnp.bfloat16).reshape(mixed.shape)
        along_y = jnp.einsum('cznx,ny->czyx', along_x.astype(jnp.float32), kernel_y.astype(jnp.float32)).astype(jnp.bfloat16)
        velocity = jnp.einsum('cnyx,nz->czyx', along_y.astype(jnp.float32), kernel_z.astype(jnp.float32)).astype(jnp.bfloat16)
        product = lax.optimization_barrier(jnp.sum(gradient * velocity.astype(jnp.float32), axis=0))
        return (total + pulled * (1.0 + product), product.astype(jnp.bfloat16))
    total, alignment = lax.scan(subject, jnp.zeros((NZ, NY, NX), jnp.float32), (momentum, padded, code))
    return (alignment, total)
```

```python
import jax
import jax.numpy as jnp
from jax import lax
from jax.sharding import PartitionSpec as P

rim = 2
bias = 8
decay = 8.0


def padded(cells, sides, width):
    for axis, dim in sides:
        count = lax.axis_size(axis)
        ends = count - 1
        head = lax.slice_in_dim(cells, 0, width, axis=dim)
        tail = lax.slice_in_dim(cells, cells.shape[dim] - width, cells.shape[dim], axis=dim)
        cells = jnp.concatenate(
            [
                lax.ppermute(tail, axis, [(i, (i + 1) % count) for i in range(ends)]),
                cells,
                lax.ppermute(head, axis, [((i + 1) % count, i) for i in range(ends)]),
            ],
            axis=dim,
        )
    return cells


def taps_matrix(rows, cols, offset):
    lags = jnp.arange(-15, 16, dtype=jnp.int32).astype(jnp.float32)
    scale = jnp.sqrt(jnp.sum(jnp.exp(-2.0 * jnp.abs(lags) / decay)))
    lag = (
        jnp.arange(rows, dtype=jnp.int32)[:, None]
        - offset
        - jnp.arange(cols, dtype=jnp.int32)[None, :]
    )
    dist = jnp.abs(lag).astype(jnp.float32)
    return jnp.where(jnp.abs(lag) <= 15, jnp.exp(-dist / decay) / scale, 0.0).astype(jnp.bfloat16)


def axis_weights(shift):
    whole = shift // 4
    frac = (shift - 4 * whole).astype(jnp.float32) * 0.25
    weights = []
    for offset in range(-rim, rim + 1):
        lower = jnp.where(whole == offset, 1.0 - frac, 0.0)
        upper = jnp.where(whole + 1 == offset, frac, 0.0)
        weights.append(lower + upper)
    return weights


def transport(framed, encoded):
    depth, height, breadth = encoded.shape
    weights_z = axis_weights(encoded // 256 - bias)
    weights_y = axis_weights(encoded // 16 % 16 - bias)
    weights_x = axis_weights(encoded % 16 - bias)
    pulled = jnp.zeros(encoded.shape, jnp.float32)
    for index_z in range(2 * rim + 1):
        plane_sum = jnp.zeros(encoded.shape, jnp.float32)
        for index_y in range(2 * rim + 1):
            row_sum = jnp.zeros(encoded.shape, jnp.float32)
            for index_x in range(2 * rim + 1):
                window = lax.slice(
                    framed,
                    (index_z, index_y, index_x),
                    (index_z + depth, index_y + height, index_x + breadth),
                )
                row_sum = row_sum + weights_x[index_x] * window.astype(jnp.float32)
            plane_sum = plane_sum + weights_y[index_y] * row_sum
        pulled = pulled + weights_z[index_z] * plane_sum
    return pulled


def per_device(momentum, adjoint, code, template_grad):
    subjects, _, depth, height, breadth = momentum.shape
    framed = padded(adjoint, (("slab", 1),), 2)
    framed = jnp.pad(framed, ((0, 0), (0, 0), (rim, rim), (rim, rim)))
    pulled = jax.vmap(transport)(framed, code)
    gradient = template_grad.astype(jnp.float32)
    mixed = (momentum.astype(jnp.float32) + pulled[:, None] * gradient[None]).astype(jnp.bfloat16)
    kernel_x = taps_matrix(breadth, breadth, 0)
    kernel_y = taps_matrix(height, height, 0)
    along_x = jnp.dot(mixed.reshape(-1, breadth), kernel_x, preferred_element_type=jnp.float32)
    along_x = along_x.astype(jnp.bfloat16).reshape(subjects * 3, depth, height, breadth)
    along_y = jnp.einsum("mznx,ny->mzyx", along_x, kernel_y, preferred_element_type=jnp.float32)
    along_y = along_y.astype(jnp.bfloat16).reshape(subjects * 3, depth, height * breadth)
    count = lax.axis_size("slab")
    blocks = along_y.reshape(3, depth, count, height * breadth // count)
    gathered = lax.all_to_all(
        blocks.transpose(2, 1, 0, 3), "slab", split_axis=0, concat_axis=0, tiled=True
    )
    planes = gathered.reshape(count * depth, 3 * (height * breadth // count))
    kernel_z = taps_matrix(count * depth, count * depth, 0)
    smooth = jnp.dot(kernel_z, planes, preferred_element_type=jnp.float32).astype(jnp.bfloat16)
    returned = lax.all_to_all(
        smooth.reshape(count, depth, 3, -1), "slab", split_axis=0, concat_axis=0, tiled=True
    )
    velocity = returned.transpose(2, 1, 0, 3)
    velocity = velocity.reshape(subjects, 3, depth, height, breadth)
    product = jnp.sum(gradient[None] * velocity.astype(jnp.float32), axis=1)
    alignment = product.astype(jnp.bfloat16)
    partial_sum = jnp.sum(pulled * (1.0 + product), axis=0)
    shares = lax.axis_size("subj")
    parts = partial_sum.reshape(depth, shares, height // shares, breadth).transpose(1, 0, 2, 3)
    template_update = jnp.sum(
        lax.all_to_all(parts, "subj", split_axis=0, concat_axis=0, tiled=True), axis=0
    )
    return (alignment, template_update)


def solution(mesh):
    return jax.shard_map(
        per_device,
        mesh=mesh,
        in_specs=(
            P("subj", None, "slab", None, None),
            P("subj", "slab", None, None),
            P("subj", "slab", None, None),
            P(None, "slab", None, None),
        ),
        out_specs=(P("subj", "slab", None, None), P("slab", "subj", None)),
        check_vma=False,
    )
```

```python
import math

import jax
import jax.numpy as jnp
from jax import lax
from jax.experimental import pallas as pl
from jax.experimental.pallas import tpu as pltpu
from jax.sharding import PartitionSpec as P

rim = 2
bias = 8
decay = 8.0
reach = 15
taps = 2 * rim + 1
lanes = 128
rows = 8
MESH = pl.DeviceIdType.MESH
scale = math.sqrt(sum(math.exp(-2.0 * abs(t) / decay) for t in range(-reach, reach + 1)))
ratio = math.exp(-1.0 / decay)


def band(size):
    lag = jnp.abs(
        lax.broadcasted_iota(jnp.int32, (size, size), 0)
        - lax.broadcasted_iota(jnp.int32, (size, size), 1)
    )
    values = jnp.exp(lag.astype(jnp.float32) * (-1.0 / decay)) / scale
    return jnp.where(lag <= reach, values, 0.0).astype(jnp.bfloat16)


def axis_weights(digit):
    place = digit.astype(jnp.float32) * 0.25 - bias * 0.25
    return [jnp.maximum(1.0 - jnp.abs(place - offset), 0.0) for offset in range(-rim, rim + 1)]


def drain(ref, sem):
    pltpu.make_async_copy(ref, ref, sem).wait()


def kernel(
    count,
    momentum,
    adjoint,
    code,
    gradient,
    alignment,
    update,
    frame,
    shifted,
    codes,
    moments,
    grads,
    pulled,
    kern,
    outgoing,
    incoming,
    far_grads,
    forward,
    backward,
    products,
    returned,
    shares,
    others,
    local_sem,
    halo_send,
    halo_recv,
    grad_send,
    grad_recv,
    swap_send,
    swap_recv,
    out_send,
    in_recv,
    back_send,
    back_recv,
    share_send,
    share_recv,
):
    subject = lax.axis_index("subj")
    slab = lax.axis_index("slab")
    subjects = others.shape[0] + 1
    components, depth, height, breadth = grads.shape
    halves = breadth // lanes
    blocks = height // rows
    partner = subject + 1 - 2 * (subject % 2)
    mine = subject % 2

    def slab_peer(step):
        hop = (step + 1) // 2
        return lax.rem(slab + count + jnp.where(step % 2 == 1, hop, -hop), count)

    barrier = pltpu.get_barrier_semaphore()

    def greet(step, carry):
        pl.semaphore_signal(
            barrier, inc=1, device_id=(subject, slab_peer(step)), device_id_type=MESH
        )
        return carry

    loads = [
        pltpu.make_async_copy(adjoint.at[0], frame.at[pl.ds(2, 2)], local_sem.at[0]),
        pltpu.make_async_copy(code.at[0], codes, local_sem.at[1]),
        pltpu.make_async_copy(momentum.at[0], moments, local_sem.at[2]),
        pltpu.make_async_copy(gradient, grads, local_sem.at[3]),
    ]
    for load in loads:
        load.start()
    lax.fori_loop(1, count, greet, 0)
    for step in range(1, subjects):
        pl.semaphore_signal(
            barrier,
            inc=1,
            device_id=(lax.rem(subject + step, subjects), slab),
            device_id_type=MESH,
        )
    kern[...] = band(max(breadth, height))
    shifted[:, :, :, pl.ds(0, rows), :] = jnp.zeros((6, taps, halves, rows, lanes), jnp.float32)
    shifted[:, :, :, pl.ds(rows + height, rows), :] = jnp.zeros(
        (6, taps, halves, rows, lanes), jnp.float32
    )
    column = lax.broadcasted_iota(jnp.int32, (height, breadth), 1)

    def spread(plane):
        values = frame[plane].astype(jnp.float32)
        for index in range(taps):
            move = index - rim
            if move == 0:
                seen = values
            else:
                turned = pltpu.roll(values, (-move) % breadth, 1)
                inside = (column + move >= 0) & (column + move < breadth)
                seen = jnp.where(inside, turned, 0.0)
            for half in range(halves):
                shifted[plane, index, half, pl.ds(rows, height), :] = seen[
                    :, half * lanes : (half + 1) * lanes
                ]

    loads[0].wait()
    pl.semaphore_wait(barrier, count - 1 + subjects - 1)

    up = pltpu.make_async_remote_copy(
        src_ref=adjoint.at[0],
        dst_ref=frame.at[pl.ds(0, 2)],
        send_sem=halo_send.at[0],
        recv_sem=halo_recv.at[0],
        device_id=(subject, lax.rem(slab + 1, count)),
        device_id_type=MESH,
    )
    down = pltpu.make_async_remote_copy(
        src_ref=adjoint.at[0],
        dst_ref=frame.at[pl.ds(4, 2)],
        send_sem=halo_send.at[1],
        recv_sem=halo_recv.at[1],
        device_id=(subject, lax.rem(slab + count - 1, count)),
        device_id_type=MESH,
    )

    up.start()
    down.start()

    def area(peer):
        return (
            pl.ds(pl.multiple_of((peer // halves) * rows, rows), rows),
            pl.ds(pl.multiple_of((peer % halves) * lanes, lanes), lanes),
        )

    def send_grad(step, carry):
        peer = slab_peer(step)
        row, col = area(peer)
        pltpu.make_async_remote_copy(
            src_ref=gradient.at[:, mine, row, col],
            dst_ref=far_grads.at[mine, slab],
            send_sem=grad_send,
            recv_sem=grad_recv,
            device_id=(subject, peer),
            device_id_type=MESH,
        ).start()
        return carry

    lax.fori_loop(1, count, send_grad, 0)
    row, col = area(slab)
    pltpu.make_async_copy(
        gradient.at[:, mine, row, col], far_grads.at[mine, slab], grad_recv
    ).start()

    spread(2)
    spread(3)
    for load in loads[1:]:
        load.wait()
    up.wait()
    down.wait()

    @pl.when(slab == 0)
    def _():
        frame[pl.ds(0, 2)] = jnp.zeros((2, height, breadth), jnp.bfloat16)

    @pl.when(slab == count - 1)
    def _():
        frame[pl.ds(4, 2)] = jnp.zeros((2, height, breadth), jnp.bfloat16)

    for plane in (0, 1, 4, 5):
        spread(plane)

    for plane in range(depth):

        def transport(block, carry):
            start = pl.multiple_of(block * rows, rows)
            for half in range(halves):
                cell = codes[plane, pl.ds(start, rows), pl.ds(half * lanes, lanes)]
                weights_z = axis_weights(cell // 256)
                weights_y = axis_weights(cell // 16 % 16)
                weights_x = axis_weights(cell % 16)
                total = None
                for index_z in range(taps):
                    plane_sum = None
                    for index_y in range(taps):
                        row_sum = None
                        for index_x in range(taps):
                            term = weights_x[index_x] * shifted[
                                plane + index_z,
                                index_x,
                                half,
                                pl.ds(start + (rows - rim + index_y), rows),
                                :,
                            ]
                            row_sum = term if row_sum is None else row_sum + term
                        term = weights_y[index_y] * row_sum
                        plane_sum = term if plane_sum is None else plane_sum + term
                    term = weights_z[index_z] * plane_sum
                    total = term if total is None else total + term
                pulled[plane, pl.ds(start, rows), pl.ds(half * lanes, lanes)] = total
            return carry

        lax.fori_loop(0, blocks, transport, 0)
        for part in range(components):
            mixed = moments[part, plane].astype(jnp.float32) + pulled[plane] * grads[
                part, plane
            ].astype(jnp.float32)
            along_x = jnp.dot(
                mixed.astype(jnp.bfloat16), kern[...], preferred_element_type=jnp.float32
            )
            along_y = jnp.dot(
                kern[:height, :height], along_x.astype(jnp.bfloat16), preferred_element_type=jnp.float32
            ).astype(jnp.bfloat16)
            for half in range(halves):
                outgoing[plane, :, half, part] = along_y[
                    :, half * lanes : (half + 1) * lanes
                ].reshape(blocks, rows, lanes)

        def send(step, carry):
            peer = slab_peer(step)
            pltpu.make_async_remote_copy(
                src_ref=outgoing.at[plane, peer // halves, peer % halves],
                dst_ref=incoming.at[plane, slab],
                send_sem=out_send.at[plane],
                recv_sem=in_recv.at[plane],
                device_id=(subject, peer),
                device_id_type=MESH,
            ).start()
            return carry

        lax.fori_loop(1, count, send, 0)
        pltpu.make_async_copy(
            outgoing.at[plane, slab // halves, slab % halves],
            incoming.at[plane, slab],
            in_recv.at[plane],
        ).start()

    drain(far_grads.at[mine], grad_recv)
    swap = pltpu.make_async_remote_copy(
        src_ref=far_grads.at[mine],
        dst_ref=far_grads.at[mine],
        send_sem=swap_send,
        recv_sem=swap_recv,
        device_id=(partner, slab),
        device_id_type=MESH,
    )
    swap.start()
    swap.wait()
    for plane in range(depth):
        drain(incoming.at[plane], in_recv.at[plane])

    gone = ratio ** (reach + 1)
    last = count - 1
    zero = jnp.zeros((components, rows, lanes), jnp.float32)
    window = (reach + 1) // depth

    def field(plane, index):
        return incoming[plane, index].astype(jnp.float32)

    def advance(with_tail):
        def step(index, carry):
            ahead, behind = carry
            mirror = last - index
            for plane in range(depth):
                ahead = ahead * ratio + field(plane, index)
                if with_tail:
                    ahead = ahead - gone * field(plane, index - window)
                forward[index, plane] = ahead
            for plane in reversed(range(depth)):
                here = field(plane, mirror)
                behind = behind * ratio + here
                if with_tail:
                    behind = behind - gone * field(plane, mirror + window)
                backward[mirror, plane] = behind - here
            return ahead, behind

        return step

    edge = min(window, count)
    carry = lax.fori_loop(0, edge, advance(False), (zero, zero))
    lax.fori_loop(edge, count, advance(True), carry)

    def combine(index, carry):
        for plane in range(depth):
            velocity = (forward[index, plane] + backward[index, plane]) * (1.0 / scale)
            slope = far_grads[plane, index].astype(jnp.float32)
            products[index, plane] = jnp.sum(slope * velocity, axis=0).astype(jnp.bfloat16)
        return carry

    lax.fori_loop(0, count, combine, 0)

    def send_back(step, carry):
        peer = slab_peer(step)
        pltpu.make_async_remote_copy(
            src_ref=products.at[peer],
            dst_ref=returned.at[slab // halves, slab % halves],
            send_sem=back_send,
            recv_sem=back_recv,
            device_id=(subject, peer),
            device_id_type=MESH,
        ).start()
        return carry

    lax.fori_loop(1, count, send_back, 0)
    pltpu.make_async_copy(
        products.at[slab], returned.at[slab // halves, slab % halves], back_recv
    ).start()
    drain(returned, back_recv)

    part_rows = height // subjects
    part_blocks = blocks // subjects

    def partial(owner, plane, half):
        block = owner * part_blocks
        values = returned[pl.ds(block, part_blocks), half, plane]
        values = values.reshape(part_rows, lanes).astype(jnp.float32)
        start = pl.multiple_of(owner * part_rows, part_rows)
        moved = pulled[plane, pl.ds(start, part_rows), pl.ds(half * lanes, lanes)]
        return moved * (1.0 + values)

    share_copies = []
    for step in range(1, subjects):
        owner = lax.rem(subject + step, subjects)
        for plane in range(depth):
            for half in range(halves):
                shares[step - 1, plane, :, pl.ds(half * lanes, lanes)] = partial(
                    owner, plane, half
                ).astype(jnp.bfloat16)
        copy = pltpu.make_async_remote_copy(
            src_ref=shares.at[step - 1],
            dst_ref=others.at[step - 1],
            send_sem=share_send.at[step - 1],
            recv_sem=share_recv.at[step - 1],
            device_id=(owner, slab),
            device_id_type=MESH,
        )
        copy.start()
        share_copies.append(copy)
    for plane in range(depth):
        for half in range(halves):
            alignment[0, plane, :, pl.ds(half * lanes, lanes)] = returned[:, half, plane].reshape(
                height, lanes
            )
    for copy in share_copies:
        copy.wait()
    for plane in range(depth):
        for half in range(halves):
            total = partial(subject, plane, half)
            for step in range(1, subjects):
                total = total + others[
                    step - 1, plane, :, pl.ds(half * lanes, lanes)
                ].astype(jnp.float32)
            update[plane, :, pl.ds(half * lanes, lanes)] = total

    sent = pl.ds(0, count - 1)
    drain(far_grads.at[0, sent], grad_send)
    for plane in range(depth):
        drain(incoming.at[0, sent], out_send.at[plane])
    drain(products.at[sent], back_send)


def solution(mesh):
    count = mesh.shape["slab"]
    subjects = mesh.shape["subj"]

    def per_device(momentum, adjoint, code, gradient):
        components, depth, height, breadth = gradient.shape
        halves = breadth // lanes
        blocks = height // rows
        part = height // subjects
        vmem, dma = pltpu.VMEM, pltpu.SemaphoreType.DMA
        half, full = jnp.bfloat16, jnp.float32

        def body(*refs):
            kernel(count, *refs)

        return pl.pallas_call(
            body,
            out_shape=(
                jax.ShapeDtypeStruct((1, depth, height, breadth), half),
                jax.ShapeDtypeStruct((depth, part, breadth), full),
            ),
            in_specs=[pl.BlockSpec(memory_space=pl.ANY)] * 4,
            out_specs=(pl.BlockSpec(memory_space=vmem), pl.BlockSpec(memory_space=vmem)),
            scratch_shapes=[
                vmem((6, height, breadth), half),
                vmem((6, taps, halves, height + 2 * rows, lanes), full),
                vmem((depth, height, breadth), jnp.int32),
                vmem((components, depth, height, breadth), half),
                vmem((components, depth, height, breadth), half),
                vmem((depth, height, breadth), full),
                vmem((breadth, breadth), half),
                vmem((depth, blocks, halves, components, rows, lanes), half),
                vmem((depth, count, components, rows, lanes), half),
                vmem((2, count, components, rows, lanes), half),
                vmem((count, depth, components, rows, lanes), full),
                vmem((count, depth, components, rows, lanes), full),
                vmem((count, depth, rows, lanes), half),
                vmem((blocks, halves, depth, rows, lanes), half),
                vmem((subjects - 1, depth, part, breadth), half),
                vmem((subjects - 1, depth, part, breadth), half),
                dma((4,)),
                dma((2,)),
                dma((2,)),
                dma,
                dma,
                dma,
                dma,
                dma((2,)),
                dma((2,)),
                dma,
                dma,
                dma((subjects - 1,)),
                dma((subjects - 1,)),
            ],
            compiler_params=pltpu.CompilerParams(
                collective_id=0, has_side_effects=True, vmem_limit_bytes=56 * 1024 * 1024
            ),
            name="step",
        )(momentum, adjoint, code, gradient)

    return jax.shard_map(
        per_device,
        mesh=mesh,
        in_specs=(
            P("subj", None, "slab", None, None),
            P("subj", "slab", None, None),
            P("subj", "slab", None, None),
            P(None, "slab", None, None),
        ),
        out_specs=(P("subj", "slab", None, None), P("slab", "subj", None)),
        check_vma=False,
    )
```

```python
import math

import jax
import jax.numpy as jnp
from jax import lax
from jax.experimental import pallas as pl
from jax.experimental.pallas import tpu as pltpu
from jax.sharding import PartitionSpec as P

rim = 2
bias = 8
decay = 8.0
reach = 15
taps = 2 * rim + 1
lanes = 128
rows = 8
MESH = pl.DeviceIdType.MESH
scale = math.sqrt(sum(math.exp(-2.0 * abs(t) / decay) for t in range(-reach, reach + 1)))
ratio = math.exp(-1.0 / decay)


def band(size):
    lag = jnp.abs(
        lax.broadcasted_iota(jnp.int32, (size, size), 0)
        - lax.broadcasted_iota(jnp.int32, (size, size), 1)
    )
    values = jnp.exp(lag.astype(jnp.float32) * (-1.0 / decay)) / scale
    return jnp.where(lag <= reach, values, 0.0).astype(jnp.bfloat16)


def position(digit):
    return digit.astype(jnp.float32) * 0.25 - bias * 0.25


def hat(distance):
    return jnp.maximum(1.0 - jnp.abs(distance), 0.0)


def axis_weights(digit):
    place = position(digit)
    return [hat(place - offset) for offset in range(-rim, rim + 1)]


def drain(ref, sem):
    pltpu.make_async_copy(ref, ref, sem).wait()


def kernel(
    count,
    momentum,
    adjoint,
    code,
    gradient,
    alignment,
    update,
    frame,
    shifted,
    codes,
    moments,
    grads,
    pulled,
    kern,
    outgoing,
    incoming,
    far_grads,
    forward,
    backward,
    products,
    returned,
    shares,
    others,
    local_sem,
    halo_send,
    halo_recv,
    grad_send,
    grad_recv,
    swap_send,
    swap_recv,
    out_send,
    in_recv,
    back_send,
    back_recv,
    share_send,
    share_recv,
):
    subject = lax.axis_index("subj")
    slab = lax.axis_index("slab")
    subjects = others.shape[0] + 1
    components, depth, height, breadth = grads.shape
    halves = breadth // lanes
    blocks = height // rows
    odd = slab % 2
    partner = subject + 1 - 2 * (subject % 2)
    across = lax.rem(subject + 2, subjects)
    group_size = count // subjects
    mine = lax.rem(subject - slab % subjects + subjects, subjects)

    def slab_peer(step):
        hop = (step + 1) // 2
        return lax.rem(slab + count + jnp.where(step % 2 == 1, hop, -hop), count)

    barrier = pltpu.get_barrier_semaphore()

    def greet(step, carry):
        pl.semaphore_signal(
            barrier, inc=1, device_id=(subject, slab_peer(step)), device_id_type=MESH
        )
        return carry

    loads = [
        pltpu.make_async_copy(adjoint.at[0], frame.at[pl.ds(2, 2)], local_sem.at[0]),
        pltpu.make_async_copy(code.at[0], codes, local_sem.at[1]),
        pltpu.make_async_copy(momentum.at[0], moments, local_sem.at[2]),
        pltpu.make_async_copy(gradient, grads, local_sem.at[3]),
    ]
    for load in loads:
        load.start()
    lax.fori_loop(1, count, greet, 0)
    for step in range(1, subjects):
        pl.semaphore_signal(
            barrier,
            inc=1,
            device_id=(lax.rem(subject + step, subjects), slab),
            device_id_type=MESH,
        )
    kern[...] = band(max(breadth, height))
    shifted[:, :, :, pl.ds(0, rows), :] = jnp.zeros((6, taps, halves, rows, lanes), jnp.float32)
    shifted[:, :, :, pl.ds(rows + height, rows), :] = jnp.zeros(
        (6, taps, halves, rows, lanes), jnp.float32
    )
    column = lax.broadcasted_iota(jnp.int32, (height, breadth), 1)

    def spread(plane):
        values = frame[plane].astype(jnp.float32)
        for index in range(taps):
            move = index - rim
            if move == 0:
                seen = values
            else:
                turned = pltpu.roll(values, (-move) % breadth, 1)
                inside = (column + move >= 0) & (column + move < breadth)
                seen = jnp.where(inside, turned, 0.0)
            for half in range(halves):
                shifted[plane, index, half, pl.ds(rows, height), :] = seen[
                    :, half * lanes : (half + 1) * lanes
                ]

    loads[0].wait()
    pl.semaphore_wait(barrier, count - 1 + subjects - 1)

    piece = height // 2
    near = (5 - 5 * odd, 4 - 3 * odd)
    far = (1 + 3 * odd, 5 * odd)
    paired = slab + 1 - 2 * odd
    onward = lax.rem(slab + 2 - 4 * odd + count, count)
    direct, passed = [], []
    for index in range(4):
        part = pl.ds((index % 2) * piece, piece)
        plane = odd if index < 2 else 1 - odd
        direct.append(
            pltpu.make_async_remote_copy(
                src_ref=adjoint.at[0, plane, part],
                dst_ref=frame.at[4 * odd + plane, part],
                send_sem=halo_send.at[index],
                recv_sem=halo_recv.at[index],
                device_id=(subject, paired),
                device_id_type=MESH,
            )
        )
        passed.append(
            pltpu.make_async_remote_copy(
                src_ref=frame.at[near[index // 2], part],
                dst_ref=frame.at[far[index // 2], part],
                send_sem=halo_send.at[4 + index],
                recv_sem=halo_recv.at[4 + index],
                device_id=(subject, onward),
                device_id_type=MESH,
            )
        )
    for copy in direct:
        copy.start()

    def area(peer):
        return (
            pl.ds(pl.multiple_of((peer // halves) * rows, rows), rows),
            pl.ds(pl.multiple_of((peer % halves) * lanes, lanes), lanes),
        )

    own_area = lax.rem(2 * slab, subjects) == subject

    def send_grad(step, carry):
        turn = lax.rem(step + slab // subjects, group_size)
        peer = mine + subjects * turn
        row, col = area(peer)
        source = gradient.at[:, :, row, col]
        target = far_grads.at[slab % subjects, slab // subjects]

        @pl.when(peer != slab)
        def _():
            pltpu.make_async_remote_copy(
                src_ref=source,
                dst_ref=target,
                send_sem=grad_send,
                recv_sem=grad_recv,
                device_id=(subject, peer),
                device_id_type=MESH,
            ).start()

        @pl.when(peer == slab)
        def _():
            pltpu.make_async_copy(source, target, grad_recv).start()

        return carry

    lax.fori_loop(0, group_size, send_grad, 0)

    def gather(plane, sources, first):
        def transport(block, carry):
            start = pl.multiple_of(block * rows, rows)
            for half in range(halves):
                cell = codes[plane, pl.ds(start, rows), pl.ds(half * lanes, lanes)]
                place_z = position(lax.shift_right_logical(cell, 8))
                weights_y = axis_weights(lax.shift_right_logical(cell, 4) & 15)
                weights_x = axis_weights(cell & 15)
                total = None
                if not first:
                    total = pulled[plane, pl.ds(start, rows), pl.ds(half * lanes, lanes)]
                for source in sources:
                    plane_sum = None
                    for index_y in range(taps):
                        row_sum = None
                        for index_x in range(taps):
                            term = weights_x[index_x] * shifted[
                                source,
                                index_x,
                                half,
                                pl.ds(start + (rows - rim + index_y), rows),
                                :,
                            ]
                            row_sum = term if row_sum is None else row_sum + term
                        term = weights_y[index_y] * row_sum
                        plane_sum = term if plane_sum is None else plane_sum + term
                    offset = jnp.asarray(source - plane - rim, jnp.int32).astype(jnp.float32)
                    term = hat(place_z - offset) * plane_sum
                    total = term if total is None else total + term
                pulled[plane, pl.ds(start, rows), pl.ds(half * lanes, lanes)] = total
            return carry

        lax.fori_loop(0, blocks, transport, 0)

    def smooth_and_send(plane):
        for part in range(components):
            mixed = moments[part, plane].astype(jnp.float32) + pulled[plane] * grads[
                part, plane
            ].astype(jnp.float32)
            along_x = jnp.dot(
                mixed.astype(jnp.bfloat16), kern[...], preferred_element_type=jnp.float32
            )
            along_y = jnp.dot(
                kern[:height, :height],
                along_x.astype(jnp.bfloat16),
                preferred_element_type=jnp.float32,
            ).astype(jnp.bfloat16)
            for half in range(halves):
                outgoing[plane, :, half, part] = along_y[
                    :, half * lanes : (half + 1) * lanes
                ].reshape(blocks, rows, lanes)

        def send(step, carry):
            peer = slab_peer(count - step)
            pltpu.make_async_remote_copy(
                src_ref=outgoing.at[plane, peer // halves, peer % halves],
                dst_ref=incoming.at[plane, slab],
                send_sem=out_send.at[plane],
                recv_sem=in_recv.at[plane],
                device_id=(subject, peer),
                device_id_type=MESH,
            ).start()
            return carry

        lax.fori_loop(1, count, send, 0)
        pltpu.make_async_copy(
            outgoing.at[plane, slab // halves, slab % halves],
            incoming.at[plane, slab],
            in_recv.at[plane],
        ).start()

    def hand_on(index):
        direct[index].wait()
        passed[index].start()

    def clear(plane):
        @pl.when((slab == 0) | (slab == count - 1))
        def _():
            frame[plane] = jnp.zeros((height, breadth), jnp.bfloat16)

    early, late = 1 - odd, odd
    spread(2)
    spread(3)
    for load in loads[1:]:
        load.wait()
    gather(0, (2, 3), True)
    hand_on(0)
    gather(1, (2, 3), True)
    hand_on(1)
    spread(near[0])
    gather(early, (near[0],), False)
    hand_on(2)
    hand_on(3)
    spread(near[1])
    gather(late, (near[1],), False)
    passed[0].wait()
    passed[1].wait()
    clear(far[0])
    spread(far[0])
    gather(early, (near[1], far[0]), False)
    smooth_and_send(early)
    passed[2].wait()
    passed[3].wait()
    clear(far[1])
    spread(far[1])
    gather(late, (far[0], far[1]), False)
    smooth_and_send(late)

    drain(far_grads.at[mine], grad_recv)
    other = lax.rem(mine + 2, subjects)

    def swap(group, index, peer):
        return pltpu.make_async_remote_copy(
            src_ref=far_grads.at[group],
            dst_ref=far_grads.at[group],
            send_sem=swap_send.at[index],
            recv_sem=swap_recv.at[index],
            device_id=(peer, slab),
            device_id_type=MESH,
        )

    swaps = [swap(mine, 0, across), swap(mine, 1, partner), swap(other, 2, partner)]
    swaps[0].start()
    swaps[1].start()
    swaps[0].wait()
    swaps[2].start()
    swaps[1].wait()
    swaps[2].wait()
    for plane in range(depth):
        drain(incoming.at[plane], in_recv.at[plane])

    gone = ratio ** (reach + 1)
    last = count - 1
    zero = jnp.zeros((components, rows, lanes), jnp.float32)
    window = (reach + 1) // depth

    def field(plane, index):
        return incoming[plane, index].astype(jnp.float32)

    def advance(with_tail):
        def step(index, carry):
            ahead, behind = carry
            mirror = last - index
            for plane in range(depth):
                ahead = ahead * ratio + field(plane, index)
                if with_tail:
                    ahead = ahead - gone * field(plane, index - window)
                forward[index, plane] = ahead
            for plane in reversed(range(depth)):
                here = field(plane, mirror)
                behind = behind * ratio + here
                if with_tail:
                    behind = behind - gone * field(plane, mirror + window)
                backward[mirror, plane] = behind - here
            return ahead, behind

        return step

    edge = min(window, count)
    carry = lax.fori_loop(0, edge, advance(False), (zero, zero))
    lax.fori_loop(edge, count, advance(True), carry)

    def combine(turn, carry):
        for group in range(subjects):
            index = turn * subjects + group
            for plane in range(depth):
                velocity = (forward[index, plane] + backward[index, plane]) * (1.0 / scale)
                slope = far_grads[group, turn, :, plane].astype(jnp.float32)
                products[index, plane] = jnp.sum(slope * velocity, axis=0).astype(jnp.bfloat16)
        return carry

    lax.fori_loop(0, group_size, combine, 0)

    def send_back(step, carry):
        peer = slab_peer(count - step)
        pltpu.make_async_remote_copy(
            src_ref=products.at[peer],
            dst_ref=returned.at[slab // halves, slab % halves],
            send_sem=back_send,
            recv_sem=back_recv.at[slab // group_size],
            device_id=(subject, peer),
            device_id_type=MESH,
        ).start()
        return carry

    lax.fori_loop(1, count, send_back, 0)
    pltpu.make_async_copy(
        products.at[slab],
        returned.at[slab // halves, slab % halves],
        back_recv.at[slab // group_size],
    ).start()

    part_rows = height // subjects
    part_blocks = blocks // subjects
    for turn in (0, 1, subjects - 1, 2):
        owner = lax.rem(slab // group_size + turn, subjects)
        band_blocks = pl.ds(owner * part_blocks, part_blocks)
        drain(returned.at[band_blocks], back_recv.at[owner])
        start = pl.multiple_of(owner * part_rows, part_rows)
        band_rows = pl.ds(start, part_rows)

        def partial(plane, half):
            values = returned[band_blocks, half, plane].reshape(part_rows, lanes)
            moved = pulled[plane, band_rows, pl.ds(half * lanes, lanes)]
            return moved * (1.0 + values.astype(jnp.float32))

        @pl.when(owner != subject)
        def _():
            slot = lax.rem(owner - subject + subjects, subjects) - 1
            for plane in range(depth):
                for half in range(halves):
                    shares[slot, plane, :, pl.ds(half * lanes, lanes)] = partial(
                        plane, half
                    ).astype(jnp.bfloat16)
            pltpu.make_async_remote_copy(
                src_ref=shares.at[slot],
                dst_ref=others.at[slot],
                send_sem=share_send.at[slot],
                recv_sem=share_recv.at[slot],
                device_id=(owner, slab),
                device_id_type=MESH,
            ).start()

        @pl.when(owner == subject)
        def _():
            for plane in range(depth):
                for half in range(halves):
                    update[plane, :, pl.ds(half * lanes, lanes)] = partial(plane, half)

        for plane in range(depth):
            for half in range(halves):
                alignment[0, plane, band_rows, pl.ds(half * lanes, lanes)] = returned[
                    band_blocks, half, plane
                ].reshape(part_rows, lanes)
    for slot in range(subjects - 1):
        drain(others.at[slot], share_recv.at[slot])
        drain(shares.at[slot], share_send.at[slot])
    update[...] = update[...] + sum(
        others[slot].astype(jnp.float32) for slot in range(subjects - 1)
    )

    sent = pl.ds(0, count - 1)
    drain(far_grads.at[0, pl.ds(0, group_size - 1)], grad_send)

    @pl.when(jnp.logical_not(own_area))
    def _():
        drain(far_grads.at[0, 0], grad_send)

    for plane in range(depth):
        drain(incoming.at[0, sent], out_send.at[plane])
    drain(products.at[sent], back_send)


def solution(mesh):
    count = mesh.shape["slab"]
    subjects = mesh.shape["subj"]

    def per_device(momentum, adjoint, code, gradient):
        components, depth, height, breadth = gradient.shape
        halves = breadth // lanes
        blocks = height // rows
        part = height // subjects
        vmem, dma = pltpu.VMEM, pltpu.SemaphoreType.DMA
        half, full = jnp.bfloat16, jnp.float32

        def body(*refs):
            kernel(count, *refs)

        return pl.pallas_call(
            body,
            out_shape=(
                jax.ShapeDtypeStruct((1, depth, height, breadth), half),
                jax.ShapeDtypeStruct((depth, part, breadth), full),
            ),
            in_specs=[pl.BlockSpec(memory_space=pl.ANY)] * 4,
            out_specs=(pl.BlockSpec(memory_space=vmem), pl.BlockSpec(memory_space=vmem)),
            scratch_shapes=[
                vmem((6, height, breadth), half),
                vmem((6, taps, halves, height + 2 * rows, lanes), full),
                vmem((depth, height, breadth), jnp.int32),
                vmem((components, depth, height, breadth), half),
                vmem((components, depth, height, breadth), half),
                vmem((depth, height, breadth), full),
                vmem((breadth, breadth), half),
                vmem((depth, blocks, halves, components, rows, lanes), half),
                vmem((depth, count, components, rows, lanes), half),
                vmem((subjects, count // subjects, components, depth, rows, lanes), half),
                vmem((count, depth, components, rows, lanes), full),
                vmem((count, depth, components, rows, lanes), full),
                vmem((count, depth, rows, lanes), half),
                vmem((blocks, halves, depth, rows, lanes), half),
                vmem((subjects - 1, depth, part, breadth), half),
                vmem((subjects - 1, depth, part, breadth), half),
                dma((4,)),
                dma((8,)),
                dma((8,)),
                dma,
                dma,
                dma((3,)),
                dma((3,)),
                dma((2,)),
                dma((2,)),
                dma,
                dma((subjects,)),
                dma((subjects - 1,)),
                dma((subjects - 1,)),
            ],
            compiler_params=pltpu.CompilerParams(
                collective_id=0, has_side_effects=True, vmem_limit_bytes=56 * 1024 * 1024
            ),
            name="step",
        )(momentum, adjoint, code, gradient)

    return jax.shard_map(
        per_device,
        mesh=mesh,
        in_specs=(
            P("subj", None, "slab", None, None),
            P("subj", "slab", None, None),
            P("subj", "slab", None, None),
            P(None, "slab", None, None),
        ),
        out_specs=(P("subj", "slab", None, None), P("slab", "subj", None)),
        check_vma=False,
    )
```
